32 devices in a mesh: prow: 8 (over z, x), pcol: 4 (over y, core).
Axes of the slice: x: 2, y: 2, z: 4, core: 2. Of those that a mesh axis runs over, the one named last changes fastest.
Arguments:
- eigvecs: float32 [16384, 2048], P('prow', 'pcol'), may hold values from -6 to 6
- reflectors: float32 [4, 16384, 256], P(None, 'prow'), may hold values from -0.046875 to 0.046875
- triangles: float32 [4, 256, 256], replicated, may hold values from -1 to 2, as said below
Outputs:
- transformed: float32 [16384, 2048], P('prow', 'pcol')
The draws below stay inside these ranges and needn't reach their ends.
Inputs may be any that keep to these rules, and one draw needn't show every extreme that they name: Each triangles[k] is upper triangular with diagonal entries between 1 and 2.
All inputs are finite; a program needn't handle non-finite values.
Results may differ from the reference program's by a relative error of at most 0.0001.
Values sent between devices are 32-bit elements; how exact they have to be, the bound alone decides.
No kernel may reach another device: no remote copies, remote signals or barrier semaphores. Data moves between devices by JAX's collectives and lax.ppermute only.
A program may use at most 128 MiB of HBM per device.

```python
import jax
import jax.numpy as jnp
from jax import lax

NB = 256
PANELS = 4
RB = 64
ROWS_DEV = 2048
ROWS = 16384
COLS = 2048
N_PROW = 8


def draw_triangles(key, part):
    first = jax.random.fold_in(key, 11)
    second = jax.random.fold_in(key, 23)
    diag_vals = jax.random.uniform(first, (PANELS, NB), jnp.float32, 1.0, 2.0)
    upper = jax.random.normal(second, (PANELS, NB, NB), jnp.float32) * (0.6 / NB ** 0.5)
    upper = jnp.clip(upper, -0.9, 0.9)
    strict = jnp.triu(jnp.ones((NB, NB), jnp.float32), 1)
    eye_mat = jnp.eye(NB, dtype=jnp.float32)
    return upper * strict[None] + diag_vals[:, :, None] * eye_mat[None]


def level_of(rng, extent, cuts, least, high):
    gain, own = 1.0, jax.random.fold_in(rng, 6)
    for dim, blocks in cuts:
        draws = jnp.exp(jax.random.uniform(jax.random.fold_in(own, dim), (blocks,), jnp.float32, least / len(cuts), high / len(cuts)))
        gain = gain * jnp.repeat(draws, extent[dim] // blocks).reshape([-1 if axis == dim else 1 for axis in range(len(extent))])
    return gain


def noise(own_key, shape, spread, limit, cuts=(), held_as=jnp.bfloat16):
    result = spread * jax.random.normal(own_key, shape, jnp.float32)
    if cuts:
        result = result * level_of(own_key, shape, cuts, -0.22, 0.18)
    return jnp.clip(result, -limit, limit).astype(held_as)


def setup_inputs(seed: int = 0) -> dict:
    key_of = jax.random.split(jax.random.key(seed), 4)
    return {
        "eigvecs": noise(key_of[0], (ROWS, COLS), 1.0, 6.0, ((0, 8), (1, 4)), jnp.float32),
        "reflectors": noise(key_of[1], (PANELS, ROWS, NB), ROWS ** -0.5, 0.046875, ((1, 8),), jnp.float32),
        "triangles": draw_triangles(jax.random.fold_in(key_of[3], 71), 0),
    }


def matrix_rows():
    stored = jnp.arange(ROWS, dtype=jnp.int32)
    owner = stored // ROWS_DEV
    local = stored % ROWS_DEV
    return ((local // RB) * N_PROW + owner) * RB + local % RB


def unit_panel(raw, index, grows):
    column = index * NB + jnp.arange(NB, dtype=jnp.int32)
    below = grows[:, None] < column[None, :]
    onto = grows[:, None] == column[None, :]
    return jnp.where(below, jnp.zeros_like(raw), jnp.where(onto, jnp.ones_like(raw), raw))


def reference(eigvecs, reflectors, triangles):
    grows = matrix_rows()
    work = eigvecs
    for index in range(PANELS):
        panel = unit_panel(reflectors[index], index, grows)
        proj = lax.dot_general(panel, work, (((0,), (0,)), ((), ())), precision=lax.Precision.HIGHEST, preferred_element_type=jnp.float32)
        coeff = jnp.dot(triangles[index], proj, precision=lax.Precision.HIGHEST, preferred_element_type=jnp.float32)
        work = work - jnp.dot(panel, coeff, precision=lax.Precision.HIGHEST, preferred_element_type=jnp.float32)
    return work
```

```python
import jax
import jax.numpy as jnp
from jax import lax
from jax.sharding import PartitionSpec as P

RB = 64


def dot(left, right, dims):
    return lax.dot_general(left, right, ((dims[:1], dims[1:]), ((), ())), precision=lax.Precision.HIGH, preferred_element_type=jnp.float32)


def inner(left, right):
    return dot(left, right, (0, 0))


def product(left, right):
    return dot(left, right, (1, 0))


def matrix_rows(rows_dev):
    owner = lax.axis_index("prow")
    local = jnp.arange(rows_dev, dtype=jnp.int32)
    return (local // RB * lax.axis_size("prow") + owner) * RB + local % RB


def unit_panel(raw, index, grows):
    column = index * raw.shape[1] + jnp.arange(raw.shape[1], dtype=jnp.int32)
    below = grows[:, None] < column[None, :]
    onto = grows[:, None] == column[None, :]
    return jnp.where(below, jnp.zeros_like(raw), jnp.where(onto, jnp.ones_like(raw), raw))


def bit_of(axis, bit):
    return (lax.axis_index(axis) >> bit) & 1


def swap(value, axis, bit):
    size = lax.axis_size(axis)
    return lax.ppermute(value, axis, [(i, i ^ (1 << bit)) for i in range(size)])


def halve(value, axis, bit):
    half = value.shape[0] // 2
    mine = bit_of(axis, bit)
    keep = lax.dynamic_slice_in_dim(value, mine * half, half, 0)
    send = lax.dynamic_slice_in_dim(value, (1 - mine) * half, half, 0)
    return keep + swap(send, axis, bit)


def join(value, axis, bit):
    other = swap(value, axis, bit)
    low = bit_of(axis, bit) == 0
    return jnp.concatenate([jnp.where(low, value, other), jnp.where(low, other, value)], 0)


def total(value, axis, order):
    bits = lax.axis_size(axis).bit_length() - 1
    for bit in order:
        value = halve(value, axis, bit)
    for bit in range(bits):
        if bit not in order:
            value = value + swap(value, axis, bit)
    for bit in reversed(order):
        value = join(value, axis, bit)
    return value


def shards(eigvecs, reflectors, triangles):
    count, _, width = reflectors.shape
    half = width // 2
    grows = matrix_rows(eigvecs.shape[0])
    stacked = jnp.concatenate([unit_panel(reflectors[k], k, grows) for k in range(count)], axis=1)
    panels = [stacked[:, k * width : (k + 1) * width] for k in range(count)]
    cut = count // 2 * width
    row_half, column_half = bit_of("pcol", 1), bit_of("pcol", 0)
    first = inner(stacked[:, :cut], eigvecs)
    pairs = []
    for k in range(1, count):
        for j in range(k):
            left = lax.dynamic_slice_in_dim(panels[k], row_half * half, half, 1)
            right = lax.dynamic_slice_in_dim(panels[j], column_half * half, half, 1)
            pairs.append(inner(left, right))
    pairs = jnp.concatenate(pairs, axis=0)
    second = inner(stacked[:, cut:], eigvecs)
    first = total(first, "prow", (0, 1))
    pairs = total(pairs, "prow", (0, 1))
    second = total(second, "prow", (1, 0))
    pairs = swap_gather(pairs, 1)
    pairs = swap_gather(pairs, 0)
    pairs = pairs.reshape(2, 2, -1, half, half)
    blocks = {}
    at = 0
    for k in range(1, count):
        for j in range(k):
            blocks[k, j] = jnp.concatenate([jnp.concatenate([pairs[0, a, at], pairs[1, a, at]], 1) for a in range(2)], 0)
            at += 1
    proj = jnp.concatenate([first, second], 0)
    coeffs = []
    for k in range(count):
        current = proj[k * width : (k + 1) * width]
        for j in range(k):
            current = current - product(blocks[k, j], coeffs[j])
        coeffs.append(product(triangles[k], current))
    work = eigvecs - product(stacked[:, :cut], jnp.concatenate(coeffs[: count // 2], axis=0))
    return work - product(stacked[:, cut:], jnp.concatenate(coeffs[count // 2 :], axis=0))


def swap_gather(value, bit):
    return join(value, "pcol", bit)


def solution(mesh):
    in_specs = (P("prow", "pcol"), P(None, "prow", None), P())
    out_specs = P("prow", "pcol")
    return jax.shard_map(shards, mesh=mesh, in_specs=in_specs, out_specs=out_specs, check_vma=False)
```

```python
import functools

import jax
import jax.numpy as jnp
from jax import lax
from jax.experimental import pallas as pl
from jax.experimental.pallas import tpu as pltpu
from jax.sharding import PartitionSpec as P


RB = 64
TILES = 4


def split(value):
    high = value.astype(jnp.bfloat16)
    return high, (value - high.astype(jnp.float32)).astype(jnp.bfloat16)


def dot3(left, right, dims=(1, 0)):
    def one(a, b):
        return lax.dot_general(a, b, ((dims[:1], dims[1:]), ((), ())), preferred_element_type=jnp.float32)

    return one(left[0], right[0]) + (one(left[0], right[1]) + one(left[1], right[0]))


def unit(raw, panel, first_row, owner, size):
    _, width = raw.shape
    local = first_row + lax.broadcasted_iota(jnp.int32, raw.shape, 0)
    grow = ((local // RB) * size + owner) * RB + local % RB
    column = panel * width + lax.broadcasted_iota(jnp.int32, raw.shape, 1)
    return jnp.where(grow < column, 0.0, jnp.where(grow == column, 1.0, raw))


def rows_of(tile, rows):
    return slice(tile * (rows // TILES), (tile + 1) * (rows // TILES))


def covered_rows(panels, width, size):
    return RB * -(-panels * width // (RB * size))


def load_split(raw, panel, rows, total_panels, owner, size):
    if rows.start < covered_rows(total_panels, raw.shape[1], size):
        raw = unit(raw, panel, rows.start, owner, size)
    return split(raw)


def emit(total, order, kk_ref, ks_ref, s_ref):
    rows = kk_ref.shape[0]
    for at, ref in enumerate((kk_ref, ks_ref, s_ref.at[0], s_ref.at[1])):
        start = pl.multiple_of((order ^ at) * rows, 8)
        ref[...] = total[pl.ds(start, rows), :]


def late_order(panel, scal):
    return scal[1 + panel % 2]


def first_kernel(size, panels, scal, w_hbm, v_hbm, kk_ref, ks_ref, s_ref, wh, wl, vh, vl, wbuf, vbuf, total, sem):
    rows, count = wbuf.shape[0], vbuf.shape[0]
    copies = []
    for t in range(TILES):
        r = rows_of(t, rows)
        copies.append(
            [pltpu.make_async_copy(w_hbm.at[r], wbuf.at[r], sem.at[0, t])]
            + [pltpu.make_async_copy(v_hbm.at[k, r], vbuf.at[k, r], sem.at[1 + k, t]) for k in range(count)]
        )
        for copy in copies[-1]:
            copy.start()
    for t in range(TILES):
        r = rows_of(t, rows)
        for copy in copies[t]:
            copy.wait()
        left = split(wbuf[r, :].T)
        wh[:, r], wl[:, r] = left
        for k in range(count):
            right = load_split(vbuf[k, r, :], k, r, panels, scal[0], size)
            vh[k, r, :], vl[k, r, :] = right
            value = dot3(left, right)
            total[k] = value if t == 0 else total[k] + value
    for k in range(count):
        emit(total.at[k], scal[2], kk_ref.at[k], ks_ref.at[k], s_ref.at[k])


def second_kernel(scal, wh, wl, vh, vl, *refs):
    total = refs[-1]
    for k in range(vh.shape[0]):
        total[k] = dot3((wh[...], wl[...]), (vh[k], vl[k]))
        emit(total.at[k], late_order(k, scal), *refs[3 * k : 3 * k + 3])


def pairs_kernel(size, scal, eh, el, v_hbm, kk_ref, ks_ref, s_ref, lh, ll, vbuf, total, sem):
    later, rows, width = vbuf.shape
    half = width // 2
    count = eh.shape[0]
    panels = count + later
    copies = []
    for t in range(TILES):
        r = rows_of(t, rows)
        copies.append([pltpu.make_async_copy(v_hbm.at[count + k, r], vbuf.at[k, r], sem.at[k, t]) for k in range(later)])
        for copy in copies[-1]:
            copy.start()
    for t in range(TILES):
        r = rows_of(t, rows)
        for copy in copies[t]:
            copy.wait()
        for k in range(later):
            lh[k, r, :], ll[k, r, :] = load_split(vbuf[k, r, :], count + k, r, panels, scal[0], size)

        def side(chosen, which):
            c = pl.ds(pl.multiple_of(which * half, half), half)
            highs = [(eh if k < count else lh)[k % count, r, c] for k in chosen]
            lows = [(el if k < count else ll)[k % count, r, c] for k in chosen]
            return jnp.concatenate(highs, 1), jnp.concatenate(lows, 1)

        for top in range(panels - 1, 0, -2):
            right_panels = [k for k in (top - 1, top) if k > 0]
            value = dot3(side(range(top), scal[4]), side(right_panels, scal[3]), (0, 0))
            for at, k in enumerate(right_panels):
                for j in range(k):
                    to = slice(pair_index(j, k) * half, (pair_index(j, k) + 1) * half)
                    part = value[j * half : (j + 1) * half, at * half : (at + 1) * half]
                    total[to, :] = part if t == 0 else total[to, :] + part
    emit(total, scal[1], kk_ref, ks_ref, s_ref)


def pair_index(j, k):
    return k * (k - 1) // 2 + j


def place(blocks, order, out):
    rows = blocks[0].shape[0]
    for at, ref in enumerate(blocks):
        out[pl.ds(pl.multiple_of((order ^ at) * rows, 8), rows), :] = ref[...]


def place_parts(scal, quarters, parts):
    rows = parts.shape[2] // 4
    for at, ref in enumerate(quarters):
        place([ref.at[pl.ds(b * rows, rows)] for b in range(4)], scal[1], parts.at[scal[3] ^ (at & 1), scal[4] ^ (at >> 1)])


def pair(parts, j, k):
    half = parts.shape[3]
    at = slice(pair_index(j, k) * half, (pair_index(j, k) + 1) * half)
    return jnp.concatenate([jnp.concatenate([parts[0, b, at, :], parts[1, b, at, :]], 1) for b in range(2)], 0)


def subtract(value, vh, vl, r, chigh, clow):
    width = vh.shape[2]
    for k in range(vh.shape[0]):
        c = slice(k * width, (k + 1) * width)
        value = value - dot3((vh[k, r, :], vl[k, r, :]), (chigh[c, :], clow[c, :]))
    return value


def blocks_at(panel, turned, mine, near0, near1, far):
    inner, outer = (near0, near1) if turned else (near1, near0)
    return [ref.at[panel] for ref in (mine, inner, outer, far)]


def middle_kernel(scal, *refs):
    mine, near0, near1, far = refs[:4]
    quarters = refs[4:8]
    tri, w_ref, vh, vl, o_ref, pre, proj, parts, chigh, clow = refs[8:]
    count, width, _ = tri.shape
    place_parts(scal, quarters, parts)
    coeffs = []
    for k in range(count):
        place(blocks_at(k, True, mine, near0, near1, far), scal[2], proj)
        current = proj[...]
        for j in range(k):
            current = current - dot3(coeffs[j], split(pair(parts, j, k)))
        coeff = dot3(split(current), split(tri[k]), (1, 1))
        coeffs.append(split(coeff))
        chigh[k * width : (k + 1) * width, :], clow[k * width : (k + 1) * width, :] = split(coeff.T)
    for k in range(count):
        value = 0.0
        for j in range(count):
            value = value + dot3(coeffs[j], split(pair(parts, j, count + k)))
        pre[k] = value
    for t in range(TILES):
        r = rows_of(t, w_ref.shape[0])
        o_ref[r, :] = subtract(w_ref[r, :], vh, vl, r, chigh, clow)


def fold_kernel(scal, q0, q1, q2, q3, tri, vh, vl, uh, ul, parts):
    count = tri.shape[0]
    place_parts(scal, (q0, q1, q2, q3), parts)
    tris = [split(tri[k]) for k in range(count)]
    for t in range(TILES):
        r = rows_of(t, vh.shape[1])
        for k in reversed(range(count)):
            value = (vh[k, r, :], vl[k, r, :])
            if k < count - 1:
                value = value[0].astype(jnp.float32) + value[1].astype(jnp.float32)
                for i in range(k + 1, count):
                    value = value - dot3((uh[i, r, :], ul[i, r, :]), split(pair(parts, count + k, count + i)), (1, 1))
                value = split(value)
            uh[k, r, :], ul[k, r, :] = split(dot3(value, tris[k]))


def last_kernel(scal, mine, near0, near1, far, pre, w_ref, uh, ul, o_hbm, proj, chigh, clow, obuf, sem):
    count, _, width = uh.shape
    for k in range(count):
        place(blocks_at(k, k % 2 == 1, mine, near0, near1, far), late_order(k, scal), proj)
        c = slice(k * width, (k + 1) * width)
        chigh[c, :], clow[c, :] = split((proj[...] - pre[k]).T)
    copies = []
    for t in range(TILES):
        r = rows_of(t, w_ref.shape[0])
        obuf[r, :] = subtract(w_ref[r, :], uh, ul, r, chigh, clow)
        copies.append(pltpu.make_async_copy(obuf.at[r], o_hbm.at[r], sem.at[t]))
        copies[-1].start()
    for copy in copies:
        copy.wait()


CHIP = pl.BlockSpec(memory_space=pltpu.VMEM)
FAR = pl.BlockSpec(memory_space=pltpu.HBM)


def call(kernel, args, in_specs, outs, out_specs, scratch, flops, limit):
    return pl.pallas_call(
        kernel,
        in_specs=[pl.BlockSpec(memory_space=pltpu.SMEM)] + in_specs,
        out_specs=out_specs,
        out_shape=outs,
        scratch_shapes=scratch,
        compiler_params=pltpu.CompilerParams(vmem_limit_bytes=limit << 20),
        cost_estimate=pl.CostEstimate(flops=flops, bytes_accessed=0, transcendentals=0),
    )(*args)


def far(value):
    return pltpu.with_memory_space_constraint(value, pltpu.HBM)


def shape(*dims, dtype=jnp.float32):
    return jax.ShapeDtypeStruct(dims, dtype)


def blocks_of(tall, wide, *lead):
    return [shape(*lead, tall // 4, wide), shape(*lead, tall // 4, wide), shape(*lead, 2, tall // 4, wide)]


def pair_of(*dims):
    return [shape(*dims, dtype=jnp.bfloat16)] * 2


def project_first(scal, eigvecs, reflectors, count):
    rows, cols = eigvecs.shape
    panels, _, width = reflectors.shape
    out = call(
        functools.partial(first_kernel, lax.axis_size("prow"), panels),
        (scal, far(eigvecs), far(reflectors)),
        [FAR, FAR],
        blocks_of(cols, width, count) + pair_of(cols, rows) + pair_of(count, rows, width),
        [CHIP] * 7,
        [
            pltpu.VMEM((rows, cols), jnp.float32),
            pltpu.VMEM((count, rows, width), jnp.float32),
            pltpu.VMEM((count, cols, width), jnp.float32),
            pltpu.SemaphoreType.DMA((1 + count, TILES)),
        ],
        6 * rows * cols * count * width,
        24,
    )
    return out[:3], out[3:5], out[5:]


def pair_products(scal, early, reflectors):
    panels, rows, width = reflectors.shape
    half = width // 2
    tall = panels * (panels - 1) // 2 * half
    later = panels - early[0].shape[0]
    out = call(
        functools.partial(pairs_kernel, lax.axis_size("prow")),
        (scal, *early, far(reflectors)),
        [CHIP, CHIP, FAR],
        blocks_of(tall, half) + pair_of(later, rows, width),
        [CHIP] * 5,
        [pltpu.VMEM((later, rows, width), jnp.float32), pltpu.VMEM((tall, half), jnp.float32), pltpu.SemaphoreType.DMA((later, TILES))],
        6 * rows * tall * half,
        16,
    )
    return out[:3], out[3:]


def project_second(scal, turned, late):
    cols, rows = turned[0].shape
    count, _, width = late[0].shape
    out = call(
        second_kernel,
        (scal, *turned, *late),
        [CHIP] * 4,
        blocks_of(cols, width) * count,
        [CHIP] * (3 * count),
        [pltpu.VMEM((count, cols, width), jnp.float32)],
        6 * rows * cols * count * width,
        12,
    )
    return [out[3 * k : 3 * k + 3] for k in range(count)]


def parts_scratch(quarters):
    return pltpu.VMEM((2, 2) + quarters[0].shape, jnp.float32)


def coeff_scratch(count, width, cols):
    return [pltpu.VMEM((count * width, cols), jnp.bfloat16)] * 2


def update_middle(scal, blocks, tri, quarters, work, early):
    rows, cols = work.shape
    count, _, width = early[0].shape
    return call(
        middle_kernel,
        (scal, *blocks, *quarters, tri, work, *early),
        [CHIP] * 12,
        [shape(rows, cols), shape(count, cols, width)],
        [CHIP] * 2,
        [pltpu.VMEM((cols, width), jnp.float32), parts_scratch(quarters)] + coeff_scratch(count, width, cols),
        6 * rows * cols * count * width,
        12,
    )


def fold(scal, quarters, tri, late):
    count, rows, width = late[0].shape
    return call(
        fold_kernel,
        (scal, *quarters, tri, *late),
        [CHIP] * 7,
        pair_of(count, rows, width),
        [CHIP] * 2,
        [parts_scratch(quarters)],
        6 * rows * width * width * 3,
        12,
    )


def update_last(scal, blocks, pre, work, folded):
    rows, cols = work.shape
    count, _, width = folded[0].shape
    return call(
        last_kernel,
        (scal, *blocks, pre, work, *folded),
        [CHIP] * 8,
        shape(rows, cols),
        FAR,
        [pltpu.VMEM((cols, width), jnp.float32)]
        + coeff_scratch(count, width, cols)
        + [pltpu.VMEM((rows, cols), jnp.float32), pltpu.SemaphoreType.DMA((TILES,))],
        6 * rows * cols * count * width,
        16,
    )


def bit_of(axis, bit):
    return (lax.axis_index(axis) >> bit) & 1


def swap(value, axis, flip):
    size = lax.axis_size(axis)
    return lax.ppermute(value, axis, [(i, i ^ flip) for i in range(size)])


def reduced(parts, outer, inner):
    keep_keep, keep_send, send = parts
    got = swap(send, "prow", outer)
    passed = keep_send + got[..., 1, :, :]
    return keep_keep, got[..., 0, :, :], swap(passed, "prow", inner)


def rest_summed(value):
    flip = 4
    while flip < lax.axis_size("prow"):
        got = swap(value, "prow", flip)
        value = value + got
        flip *= 2
    return value


def one_reduced(parts, outer, inner):
    a, b, c = reduced(parts, outer, inner)
    value = a + b + c
    return rest_summed(value)


def two_reduced(even, odd):
    even, odd = reduced(even, 1, 2), reduced(odd, 2, 1)
    value = jnp.stack([a + b + c for a, b, c in (even, odd)])
    return rest_summed(value)


def shared(value):
    return swap(value, "prow", 1), swap(value, "prow", 2)


def body(eigvecs, reflectors, triangles):
    panels = reflectors.shape[0]
    count = panels // 2
    low, high = bit_of("prow", 0), bit_of("prow", 1)
    scal = jnp.stack([lax.axis_index("prow"), low * 2 + high, high * 2 + low, bit_of("pcol", 1), bit_of("pcol", 0)]).astype(jnp.int32)

    first, turned, early = project_first(scal, eigvecs, reflectors, count)
    pairs, late = pair_products(scal, early, reflectors)
    second = project_second(scal, turned, late)
    pairs = one_reduced(pairs, 1, 2)
    near0, near1 = shared(pairs)
    diag = swap(pairs, "prow", 3)
    pairs = jnp.concatenate([pairs, near1, near0, diag], 0)
    across = swap(pairs, "pcol", 2)
    quarters = (pairs, across, swap(pairs, "pcol", 1), swap(across, "pcol", 1))
    mine = one_reduced(first, 2, 1)
    near0, near1 = shared(mine)
    work, pre = update_middle(scal, (mine, near0, near1, swap(near0, "prow", 2)), triangles[:count], quarters, eigvecs, early)
    folded = fold(scal, quarters, triangles[count:], late)
    mine = two_reduced(*second)
    return update_last(scal, (mine, *shared(mine), swap(mine, "prow", 3)), pre, work, folded)


def solution(mesh):
    in_specs = (P("prow", "pcol"), P(None, "prow", None), P())
    out_specs = P("prow", "pcol")
    return jax.shard_map(body, mesh=mesh, in_specs=in_specs, out_specs=out_specs, check_vma=False)
```

```python
import functools

import jax
import jax.numpy as jnp
from jax import lax
from jax.experimental import pallas as pl
from jax.experimental.pallas import tpu as pltpu
from jax.sharding import PartitionSpec as P


RB = 64
TILES = 8


def split(value):
    high = value.astype(jnp.bfloat16)
    return high, (value - high.astype(jnp.float32)).astype(jnp.bfloat16)


def dot3(left, right, dims=(1, 0)):
    def one(a, b):
        return lax.dot_general(a, b, ((dims[:1], dims[1:]), ((), ())), preferred_element_type=jnp.float32)

    return one(left[0], right[0]) + (one(left[0], right[1]) + one(left[1], right[0]))


def unit(raw, panel, first_row, owner, size):
    _, width = raw.shape
    local = first_row + lax.broadcasted_iota(jnp.int32, raw.shape, 0)
    grow = ((local // RB) * size + owner) * RB + local % RB
    column = panel * width + lax.broadcasted_iota(jnp.int32, raw.shape, 1)
    return jnp.where(grow < column, 0.0, jnp.where(grow == column, 1.0, raw))


def rows_of(tile, rows):
    return slice(tile * (rows // TILES), (tile + 1) * (rows // TILES))


def covered_rows(panels, width, size):
    return RB * -(-panels * width // (RB * size))


def load_split(raw, panel, rows, total_panels, owner, size):
    if rows.start < covered_rows(total_panels, raw.shape[1], size):
        raw = unit(raw, panel, rows.start, owner, size)
    return split(raw)


def emit(total, order, kk_ref, ks_ref, s_ref):
    rows = kk_ref.shape[0]
    for at, ref in enumerate((kk_ref, ks_ref, s_ref.at[0], s_ref.at[1])):
        start = pl.multiple_of((order ^ at) * rows, 8)
        ref[...] = total[pl.ds(start, rows), :]


def late_order(panel, scal):
    return scal[1 + panel % 2]


def first_kernel(size, scal, w_hbm, v_hbm, kk_ref, ks_ref, s_ref, wh, wl, eh, el, lh, ll, wbuf, vbuf, total, sem):
    panels, rows, width = vbuf.shape
    count = eh.shape[1] // width

    def fetch(k, t):
        r = rows_of(t, rows)
        if k < 0:
            return pltpu.make_async_copy(w_hbm.at[r], wbuf.at[r], sem.at[panels, t])
        return pltpu.make_async_copy(v_hbm.at[k, r], vbuf.at[k, r], sem.at[k, t])

    early = [[fetch(k, t) for k in range(-1, count)] for t in range(TILES)]
    late = [[fetch(k, t) for k in range(count, panels)] for t in range(TILES)]
    for copies in early + late:
        for copy in copies:
            copy.start()
    for t in range(TILES):
        r = rows_of(t, rows)
        for copy in early[t]:
            copy.wait()
        left = split(wbuf[r, :].T)
        wh[:, r], wl[:, r] = left
        for k in range(count):
            right = load_split(vbuf[k, r, :], k, r, panels, scal[0], size)
            c = slice(k * width, (k + 1) * width)
            eh[r, c], el[r, c] = right
            value = dot3(left, right)
            total[k] = value if t == 0 else total[k] + value
    for k in range(count):
        emit(total.at[k], scal[2], kk_ref.at[k], ks_ref.at[k], s_ref.at[k])
    for t in range(TILES):
        r = rows_of(t, rows)
        for copy in late[t]:
            copy.wait()
        for k in range(count, panels):
            c = slice((k - count) * width, (k - count + 1) * width)
            lh[r, c], ll[r, c] = load_split(vbuf[k, r, :], k, r, panels, scal[0], size)


def second_kernel(scal, wh, wl, vh, vl, *refs):
    for k in range(len(refs) // 3):
        kk_ref, ks_ref, s_ref = refs[3 * k : 3 * k + 3]
        rows, width = kk_ref.shape
        c = slice(k * width, (k + 1) * width)
        at = [pl.ds(pl.multiple_of((late_order(k, scal) ^ b) * rows, rows), rows) for b in range(4)]
        left = [jnp.concatenate([ref[b, :] for b in at], 0) for ref in (wh, wl)]
        value = dot3(left, (vh[:, c], vl[:, c]))
        kk_ref[...], ks_ref[...] = value[:rows], value[rows : 2 * rows]
        s_ref[0], s_ref[1] = value[2 * rows : 3 * rows], value[3 * rows :]


def pairs_kernel(count, scal, eh, el, lh, ll, kk_ref, ks_ref, s_ref, total):
    half = total.shape[1]
    panels = 2 * count

    def columns(k, which):
        return pl.ds(pl.multiple_of((2 * (k % count) + which) * half, half), half)

    def side(chosen, which):
        highs = [(eh if k < count else lh)[:, columns(k, which)] for k in chosen]
        lows = [(el if k < count else ll)[:, columns(k, which)] for k in chosen]
        return jnp.concatenate(highs, 1), jnp.concatenate(lows, 1)

    for top in range(panels - 1, 0, -2):
        right_panels = [k for k in (top - 1, top) if k > 0]
        value = dot3(side(range(top), scal[4]), side(right_panels, scal[3]), (0, 0))
        for at, k in enumerate(right_panels):
            for j in range(k):
                to = slice(pair_index(j, k) * half, (pair_index(j, k) + 1) * half)
                total[to, :] = value[j * half : (j + 1) * half, at * half : (at + 1) * half]
    emit(total, scal[1], kk_ref, ks_ref, s_ref)


def pair_index(j, k):
    return k * (k - 1) // 2 + j


def place(blocks, order, out):
    rows = blocks[0].shape[0]
    for at, ref in enumerate(blocks):
        out[pl.ds(pl.multiple_of((order ^ at) * rows, 8), rows), :] = ref[...]


def place_parts(scal, quarters, parts):
    rows = parts.shape[2] // 4
    for at, ref in enumerate(quarters):
        place([ref.at[pl.ds(b * rows, rows)] for b in range(4)], scal[1], parts.at[scal[3] ^ (at & 1), scal[4] ^ (at >> 1)])


def pair(parts, j, k):
    half = parts.shape[3]
    at = slice(pair_index(j, k) * half, (pair_index(j, k) + 1) * half)
    return jnp.concatenate([jnp.concatenate([parts[0, b, at, :], parts[1, b, at, :]], 1) for b in range(2)], 0)


def subtract(value, vh, vl, r, coeff):
    return value - dot3((vh[r, :], vl[r, :]), coeff)


def blocks_at(panel, turned, mine, near0, near1, far):
    inner, outer = (near0, near1) if turned else (near1, near0)
    return [ref.at[panel] for ref in (mine, inner, outer, far)]


def fold_kernel(count, scal, q0, q1, q2, q3, tri, vh, vl, uh, ul, ph, plow, rh, rl, parts):
    width = tri.shape[2]
    place_parts(scal, (q0, q1, q2, q3), parts)
    ph[...], plow[...] = split(pair(parts, 0, 1))
    for j in range(count):
        for k in range(count):
            to = (slice(j * width, (j + 1) * width), slice(k * width, (k + 1) * width))
            rh[to], rl[to] = split(pair(parts, j, count + k))
    first, second = split(tri[0]), split(tri[1])
    cross = dot3(second, split(pair(parts, count, count + 1)), (1, 1))
    cross = dot3(split(cross), first)
    mixed = split(jnp.concatenate([tri[0], -cross], 0))
    for t in range(TILES):
        r = rows_of(t, vh.shape[0])
        uh[r, :width], ul[r, :width] = split(dot3((vh[r, :], vl[r, :]), mixed))
        uh[r, width:], ul[r, width:] = split(dot3((vh[r, width:], vl[r, width:]), second))


def middle_kernel(scal, mine, near0, near1, far, tri, ph, plow, rh, rl, w_ref, vh, vl, o_ref, pre, proj):
    for k in range(2):
        place(blocks_at(k, True, mine, near0, near1, far), scal[2], proj.at[k])
    first = dot3(split(proj[0]), split(tri[0]), (1, 1))
    second = proj[1] - dot3(split(first), (ph[...], plow[...]))
    second = dot3(split(second), split(tri[1]), (1, 1))
    coeff = jnp.concatenate([first, second], 1)
    turned = split(coeff.T)
    pre[...] = dot3(split(coeff), (rh[...], rl[...]))
    for t in range(TILES):
        r = rows_of(t, w_ref.shape[0])
        o_ref[r, :] = subtract(w_ref[r, :], vh, vl, r, turned)


def last_kernel(scal, mine, near0, near1, far, pre, w_ref, uh, ul, o_hbm, proj, obuf, sem):
    count, _, _ = proj.shape
    for k in range(count):
        place(blocks_at(k, k % 2 == 1, mine, near0, near1, far), late_order(k, scal), proj.at[k])
    turned = split((jnp.concatenate([proj[k] for k in range(count)], 1) - pre[...]).T)
    copies = []
    steps = sem.shape[0]
    for t in range(steps):
        tall = w_ref.shape[0] // steps
        r = slice(t * tall, (t + 1) * tall)
        obuf[r, :] = subtract(w_ref[r, :], uh, ul, r, turned)
        copies.append(pltpu.make_async_copy(obuf.at[r], o_hbm.at[r], sem.at[t]))
        copies[-1].start()
    for copy in copies:
        copy.wait()


CHIP = pl.BlockSpec(memory_space=pltpu.VMEM)
FAR = pl.BlockSpec(memory_space=pltpu.HBM)


def call(kernel, args, in_specs, outs, out_specs, scratch, flops, limit):
    return pl.pallas_call(
        kernel,
        in_specs=[pl.BlockSpec(memory_space=pltpu.SMEM)] + in_specs,
        out_specs=out_specs,
        out_shape=outs,
        scratch_shapes=scratch,
        compiler_params=pltpu.CompilerParams(vmem_limit_bytes=limit << 20),
        cost_estimate=pl.CostEstimate(flops=flops, bytes_accessed=0, transcendentals=0),
    )(*args)


def far(value):
    return pltpu.with_memory_space_constraint(value, pltpu.HBM)


def shape(*dims, dtype=jnp.float32):
    return jax.ShapeDtypeStruct(dims, dtype)


def blocks_of(tall, wide, *lead):
    return [shape(*lead, tall // 4, wide), shape(*lead, tall // 4, wide), shape(*lead, 2, tall // 4, wide)]


def pair_of(*dims):
    return [shape(*dims, dtype=jnp.bfloat16)] * 2


def project_first(scal, eigvecs, reflectors, count):
    rows, cols = eigvecs.shape
    panels, _, width = reflectors.shape
    out = call(
        functools.partial(first_kernel, lax.axis_size("prow")),
        (scal, far(eigvecs), far(reflectors)),
        [FAR, FAR],
        blocks_of(cols, width, count) + pair_of(cols, rows) + pair_of(rows, count * width) + pair_of(rows, (panels - count) * width),
        [CHIP] * 9,
        [
            pltpu.VMEM((rows, cols), jnp.float32),
            pltpu.VMEM((panels, rows, width), jnp.float32),
            pltpu.VMEM((count, cols, width), jnp.float32),
            pltpu.SemaphoreType.DMA((panels + 1, TILES)),
        ],
        6 * rows * cols * count * width,
        24,
    )
    return out[:3], out[3:5], out[5:7], out[7:]


def pair_products(scal, early, late, width):
    rows, wide = early[0].shape
    count = wide // width
    half = width // 2
    tall = count * (2 * count - 1) * half
    return call(
        functools.partial(pairs_kernel, count),
        (scal, *early, *late),
        [CHIP] * 4,
        blocks_of(tall, half),
        [CHIP] * 3,
        [pltpu.VMEM((tall, half), jnp.float32)],
        6 * rows * tall * half,
        16,
    )


def project_second(scal, turned, late, width):
    cols, rows = turned[0].shape
    count = late[0].shape[1] // width
    out = call(
        second_kernel,
        (scal, *turned, *late),
        [CHIP] * 4,
        blocks_of(cols, width) * count,
        [CHIP] * (3 * count),
        [],
        6 * rows * cols * count * width,
        12,
    )
    return [out[3 * k : 3 * k + 3] for k in range(count)]


def fold(scal, quarters, tri, late):
    rows, wide = late[0].shape
    count, width, _ = tri.shape
    out = call(
        functools.partial(fold_kernel, count),
        (scal, *quarters, tri, *late),
        [CHIP] * 7,
        pair_of(rows, wide) + pair_of(width, width) + pair_of(wide, wide),
        [CHIP] * 6,
        [pltpu.VMEM((2, 2) + quarters[0].shape, jnp.float32)],
        6 * rows * width * width * 3,
        12,
    )
    return out[:2], out[2:]


def update_middle(scal, blocks, tri, joined, work, early):
    rows, cols = work.shape
    count, width, _ = tri.shape
    return call(
        middle_kernel,
        (scal, *blocks, tri, *joined, work, *early),
        [CHIP] * 12,
        [shape(rows, cols), shape(cols, count * width)],
        [CHIP] * 2,
        [pltpu.VMEM((count, cols, width), jnp.float32)],
        6 * rows * cols * count * width,
        12,
    )


def update_last(scal, blocks, pre, work, folded):
    rows, cols = work.shape
    count, width = blocks[0].shape[0], blocks[0].shape[2]
    return call(
        last_kernel,
        (scal, *blocks, pre, work, *folded),
        [CHIP] * 8,
        shape(rows, cols),
        FAR,
        [pltpu.VMEM((count, cols, width), jnp.float32), pltpu.VMEM((rows, cols), jnp.float32), pltpu.SemaphoreType.DMA((2 * TILES,))],
        6 * rows * cols * count * width,
        16,
    )


def bit_of(axis, bit):
    return (lax.axis_index(axis) >> bit) & 1


def swap(value, axis, flip):
    size = lax.axis_size(axis)
    return lax.ppermute(value, axis, [(i, i ^ flip) for i in range(size)])


def reduced(parts, outer, inner):
    keep_keep, keep_send, send = parts
    got = swap(send, "prow", outer)
    passed = keep_send + got[..., 1, :, :]
    return keep_keep, got[..., 0, :, :], swap(passed, "prow", inner)


def rest_summed(value):
    flip = 4
    while flip < lax.axis_size("prow"):
        got = swap(value, "prow", flip)
        value = value + got
        flip *= 2
    return value


def one_reduced(parts, outer, inner):
    a, b, c = reduced(parts, outer, inner)
    value = a + b + c
    return rest_summed(value)


def two_reduced(even, odd):
    even, odd = reduced(even, 1, 2), reduced(odd, 2, 1)
    value = jnp.stack([a + b + c for a, b, c in (even, odd)])
    return rest_summed(value)


def shared(value):
    return swap(value, "prow", 1), swap(value, "prow", 2)


def body(eigvecs, reflectors, triangles):
    panels, _, width = reflectors.shape
    count = panels // 2
    low, high = bit_of("prow", 0), bit_of("prow", 1)
    scal = jnp.stack([lax.axis_index("prow"), low * 2 + high, high * 2 + low, bit_of("pcol", 1), bit_of("pcol", 0)]).astype(jnp.int32)

    first, turned, early, late = project_first(scal, eigvecs, reflectors, count)
    pairs = pair_products(scal, early, late, width)
    second = project_second(scal, turned, late, width)
    pairs = one_reduced(pairs, 1, 2)
    near0, near1 = shared(pairs)
    diag = swap(pairs, "prow", 3)
    pairs = jnp.concatenate([pairs, near1, near0, diag], 0)
    across = swap(pairs, "pcol", 2)
    quarters = (pairs, across, swap(pairs, "pcol", 1), swap(across, "pcol", 1))
    mine = one_reduced(first, 2, 1)
    near0, near1 = shared(mine)
    folded, joined = fold(scal, quarters, triangles[count:], late)
    blocks = (mine, near0, near1, swap(mine, "prow", 3))
    work, pre = update_middle(scal, blocks, triangles[:count], joined, eigvecs, early)
    mine = two_reduced(*second)
    return update_last(scal, (mine, *shared(mine), swap(mine, "prow", 3)), pre, work, folded)


def solution(mesh):
    in_specs = (P("prow", "pcol"), P(None, "prow", None), P())
    out_specs = P("prow", "pcol")
    return jax.shard_map(body, mesh=mesh, in_specs=in_specs, out_specs=out_specs, check_vma=False)
```

```python
import functools

import jax
import jax.numpy as jnp
from jax import lax
from jax.experimental import pallas as pl
from jax.experimental.pallas import tpu as pltpu
from jax.sharding import PartitionSpec as P


RB = 64
TILES = 4


def split(value):
    high = value.astype(jnp.bfloat16)
    return high, (value - high.astype(jnp.float32)).astype(jnp.bfloat16)


def dot3(left, right, dims=(1, 0)):
    def one(a, b):
        return lax.dot_general(a, b, ((dims[:1], dims[1:]), ((), ())), preferred_element_type=jnp.float32)

    return one(left[0], right[0]) + (one(left[0], right[1]) + one(left[1], right[0]))


def unit(raw, panel, first_row, owner, size):
    _, width = raw.shape
    local = first_row + lax.broadcasted_iota(jnp.int32, raw.shape, 0)
    grow = ((local // RB) * size + owner) * RB + local % RB
    column = panel * width + lax.broadcasted_iota(jnp.int32, raw.shape, 1)
    return jnp.where(grow < column, 0.0, jnp.where(grow == column, 1.0, raw))


def rows_of(tile, rows):
    return slice(tile * (rows // TILES), (tile + 1) * (rows // TILES))


def covered_rows(panels, width, size):
    return RB * -(-panels * width // (RB * size))


def load_split(raw, panel, rows, total_panels, owner, size):
    if rows.start < covered_rows(total_panels, raw.shape[1], size):
        raw = unit(raw, panel, rows.start, owner, size)
    return split(raw)


def emit(total, order, kk_ref, ks_ref, s_ref):
    rows = kk_ref.shape[0]
    for at, ref in enumerate((kk_ref, ks_ref, s_ref.at[0], s_ref.at[1])):
        start = pl.multiple_of((order ^ at) * rows, 8)
        ref[...] = total[pl.ds(start, rows), :]


def late_order(panel, scal):
    return scal[1 + panel % 2]


def first_kernel(size, scal, w_hbm, v_hbm, kk_ref, ks_ref, s_ref, wh, wl, eh, el, lh, ll, wbuf, vbuf, total, sem):
    panels, rows, width = vbuf.shape
    count = eh.shape[1] // width

    def fetch(k, t):
        r = rows_of(t, rows)
        if k < 0:
            return pltpu.make_async_copy(w_hbm.at[r], wbuf.at[r], sem.at[panels, t])
        return pltpu.make_async_copy(v_hbm.at[k, r], vbuf.at[k, r], sem.at[k, t])

    early = [[fetch(k, t) for k in range(-1, count)] for t in range(TILES)]
    late = [[fetch(k, t) for k in range(count, panels)] for t in range(TILES)]
    for copies in early:
        for copy in copies:
            copy.start()
    for t in range(TILES):
        r = rows_of(t, rows)
        for copy in early[t]:
            copy.wait()
        for copy in late[t]:
            copy.start()
        left = split(wbuf[r, :].T)
        wh[:, r], wl[:, r] = left
        for k in range(count):
            right = load_split(vbuf[k, r, :], k, r, panels, scal[0], size)
            c = slice(k * width, (k + 1) * width)
            eh[r, c], el[r, c] = right
            value = dot3(left, right)
            total[k] = value if t == 0 else total[k] + value
    for k in range(count):
        emit(total.at[k], scal[2], kk_ref.at[k], ks_ref.at[k], s_ref.at[k])
    for t in range(TILES):
        r = rows_of(t, rows)
        for copy in late[t]:
            copy.wait()
        for k in range(count, panels):
            c = slice((k - count) * width, (k - count + 1) * width)
            lh[r, c], ll[r, c] = load_split(vbuf[k, r, :], k, r, panels, scal[0], size)


def second_kernel(scal, wh, wl, vh, vl, *refs):
    for k in range(len(refs) // 3):
        kk_ref, ks_ref, s_ref = refs[3 * k : 3 * k + 3]
        rows, width = kk_ref.shape
        c = slice(k * width, (k + 1) * width)
        at = [pl.ds(pl.multiple_of((late_order(k, scal) ^ b) * rows, rows), rows) for b in range(4)]
        left = [jnp.concatenate([ref[b, :] for b in at], 0) for ref in (wh, wl)]
        value = dot3(left, (vh[:, c], vl[:, c]))
        kk_ref[...], ks_ref[...] = value[:rows], value[rows : 2 * rows]
        s_ref[0], s_ref[1] = value[2 * rows : 3 * rows], value[3 * rows :]


def pairs_kernel(count, scal, eh, el, lh, ll, kk_ref, ks_ref, s_ref, total):
    half = total.shape[1]
    panels = 2 * count

    def columns(k, which):
        return pl.ds(pl.multiple_of((2 * (k % count) + which) * half, half), half)

    def side(chosen, which):
        highs = [(eh if k < count else lh)[:, columns(k, which)] for k in chosen]
        lows = [(el if k < count else ll)[:, columns(k, which)] for k in chosen]
        return jnp.concatenate(highs, 1), jnp.concatenate(lows, 1)

    for top in range(panels - 1, 0, -2):
        right_panels = [k for k in (top - 1, top) if k > 0]
        value = dot3(side(range(top), scal[4]), side(right_panels, scal[3]), (0, 0))
        for at, k in enumerate(right_panels):
            for j in range(k):
                to = slice(pair_index(j, k) * half, (pair_index(j, k) + 1) * half)
                total[to, :] = value[j * half : (j + 1) * half, at * half : (at + 1) * half]
    emit(total, scal[1], kk_ref, ks_ref, s_ref)


def pair_index(j, k):
    return k * (k - 1) // 2 + j


def place(blocks, order, out):
    rows = blocks[0].shape[0]
    for at, ref in enumerate(blocks):
        out[pl.ds(pl.multiple_of((order ^ at) * rows, 8), rows), :] = ref[...]


def place_parts(scal, quarters, parts):
    rows = parts.shape[2] // 4
    for at, ref in enumerate(quarters):
        place([ref.at[pl.ds(b * rows, rows)] for b in range(4)], scal[1], parts.at[scal[3] ^ (at & 1), scal[4] ^ (at >> 1)])


def pair(parts, j, k):
    half = parts.shape[3]
    at = slice(pair_index(j, k) * half, (pair_index(j, k) + 1) * half)
    return jnp.concatenate([jnp.concatenate([parts[0, b, at, :], parts[1, b, at, :]], 1) for b in range(2)], 0)


def subtract(value, vh, vl, r, coeff):
    return value - dot3((vh[r, :], vl[r, :]), coeff)


def blocks_at(panel, turned, mine, near0, near1, far):
    inner, outer = (near0, near1) if turned else (near1, near0)
    return [ref.at[panel] for ref in (mine, inner, outer, far)]


def fold_kernel(count, scal, q0, q1, q2, q3, tri, vh, vl, uh, ul, ph, plow, rh, rl, parts):
    width = tri.shape[2]
    place_parts(scal, (q0, q1, q2, q3), parts)
    ph[...], plow[...] = split(pair(parts, 0, 1))
    for j in range(count):
        for k in range(count):
            to = (slice(j * width, (j + 1) * width), slice(k * width, (k + 1) * width))
            rh[to], rl[to] = split(pair(parts, j, count + k))
    first, second = split(tri[0]), split(tri[1])
    cross = dot3(second, split(pair(parts, count, count + 1)), (1, 1))
    cross = dot3(split(cross), first)
    mixed = split(jnp.concatenate([tri[0], -cross], 0))
    for t in range(TILES):
        r = rows_of(t, vh.shape[0])
        uh[r, :width], ul[r, :width] = split(dot3((vh[r, :], vl[r, :]), mixed))
        uh[r, width:], ul[r, width:] = split(dot3((vh[r, width:], vl[r, width:]), second))


def middle_kernel(scal, mine, near0, near1, far, tri, ph, plow, rh, rl, w_ref, vh, vl, o_ref, pre, proj):
    for k in range(2):
        place(blocks_at(k, True, mine, near0, near1, far), scal[2], proj.at[k])
    first = dot3(split(proj[0]), split(tri[0]), (1, 1))
    second = proj[1] - dot3(split(first), (ph[...], plow[...]))
    second = dot3(split(second), split(tri[1]), (1, 1))
    coeff = jnp.concatenate([first, second], 1)
    turned = split(coeff.T)
    pre[...] = dot3(split(coeff), (rh[...], rl[...]))
    for t in range(TILES):
        r = rows_of(t, w_ref.shape[0])
        o_ref[r, :] = subtract(w_ref[r, :], vh, vl, r, turned)


def last_kernel(scal, mine, near0, near1, far, pre, w_ref, uh, ul, o_hbm, proj, obuf, sem):
    count, _, _ = proj.shape
    for k in range(count):
        place(blocks_at(k, k % 2 == 1, mine, near0, near1, far), late_order(k, scal), proj.at[k])
    turned = split((jnp.concatenate([proj[k] for k in range(count)], 1) - pre[...]).T)
    copies = []
    steps = sem.shape[0]
    for t in range(steps):
        tall = w_ref.shape[0] // steps
        r = slice(t * tall, (t + 1) * tall)
        obuf[r, :] = subtract(w_ref[r, :], uh, ul, r, turned)
        copies.append(pltpu.make_async_copy(obuf.at[r], o_hbm.at[r], sem.at[t]))
        copies[-1].start()
    for copy in copies:
        copy.wait()


CHIP = pl.BlockSpec(memory_space=pltpu.VMEM)
FAR = pl.BlockSpec(memory_space=pltpu.HBM)


def call(kernel, args, in_specs, outs, out_specs, scratch, flops, limit):
    return pl.pallas_call(
        kernel,
        in_specs=[pl.BlockSpec(memory_space=pltpu.SMEM)] + in_specs,
        out_specs=out_specs,
        out_shape=outs,
        scratch_shapes=scratch,
        compiler_params=pltpu.CompilerParams(vmem_limit_bytes=limit << 20),
        cost_estimate=pl.CostEstimate(flops=flops, bytes_accessed=0, transcendentals=0),
    )(*args)


def far(value):
    return pltpu.with_memory_space_constraint(value, pltpu.HBM)


def shape(*dims, dtype=jnp.float32):
    return jax.ShapeDtypeStruct(dims, dtype)


def blocks_of(tall, wide, *lead):
    return [shape(*lead, tall // 4, wide), shape(*lead, tall // 4, wide), shape(*lead, 2, tall // 4, wide)]


def pair_of(*dims):
    return [shape(*dims, dtype=jnp.bfloat16)] * 2


def project_first(scal, eigvecs, reflectors, count):
    rows, cols = eigvecs.shape
    panels, _, width = reflectors.shape
    out = call(
        functools.partial(first_kernel, lax.axis_size("prow")),
        (scal, far(eigvecs), far(reflectors)),
        [FAR, FAR],
        blocks_of(cols, width, count) + pair_of(cols, rows) + pair_of(rows, count * width) + pair_of(rows, (panels - count) * width),
        [CHIP] * 9,
        [
            pltpu.VMEM((rows, cols), jnp.float32),
            pltpu.VMEM((panels, rows, width), jnp.float32),
            pltpu.VMEM((count, cols, width), jnp.float32),
            pltpu.SemaphoreType.DMA((panels + 1, TILES)),
        ],
        6 * rows * cols * count * width,
        24,
    )
    return out[:3], out[3:5], out[5:7], out[7:]


def pair_products(scal, early, late, width):
    rows, wide = early[0].shape
    count = wide // width
    half = width // 2
    tall = count * (2 * count - 1) * half
    return call(
        functools.partial(pairs_kernel, count),
        (scal, *early, *late),
        [CHIP] * 4,
        blocks_of(tall, half),
        [CHIP] * 3,
        [pltpu.VMEM((tall, half), jnp.float32)],
        6 * rows * tall * half,
        16,
    )


def project_second(scal, turned, late, width):
    cols, rows = turned[0].shape
    count = late[0].shape[1] // width
    out = call(
        second_kernel,
        (scal, *turned, *late),
        [CHIP] * 4,
        blocks_of(cols, width) * count,
        [CHIP] * (3 * count),
        [],
        6 * rows * cols * count * width,
        12,
    )
    return [out[3 * k : 3 * k + 3] for k in range(count)]


def fold(scal, quarters, tri, late):
    rows, wide = late[0].shape
    count, width, _ = tri.shape
    out = call(
        functools.partial(fold_kernel, count),
        (scal, *quarters, tri, *late),
        [CHIP] * 7,
        pair_of(rows, wide) + pair_of(width, width) + pair_of(wide, wide),
        [CHIP] * 6,
        [pltpu.VMEM((2, 2) + quarters[0].shape, jnp.float32)],
        6 * rows * width * width * 3,
        12,
    )
    return out[:2], out[2:]


def update_middle(scal, blocks, tri, joined, work, early):
    rows, cols = work.shape
    count, width, _ = tri.shape
    return call(
        middle_kernel,
        (scal, *blocks, tri, *joined, work, *early),
        [CHIP] * 12,
        [shape(rows, cols), shape(cols, count * width)],
        [CHIP] * 2,
        [pltpu.VMEM((count, cols, width), jnp.float32)],
        6 * rows * cols * count * width,
        12,
    )


def update_last(scal, blocks, pre, work, folded):
    rows, cols = work.shape
    count, width = blocks[0].shape[0], blocks[0].shape[2]
    return call(
        last_kernel,
        (scal, *blocks, pre, work, *folded),
        [CHIP] * 8,
        shape(rows, cols),
        FAR,
        [pltpu.VMEM((count, cols, width), jnp.float32), pltpu.VMEM((rows, cols), jnp.float32), pltpu.SemaphoreType.DMA((2 * TILES,))],
        6 * rows * cols * count * width,
        16,
    )


def bit_of(axis, bit):
    return (lax.axis_index(axis) >> bit) & 1


def swap(value, axis, flip):
    size = lax.axis_size(axis)
    return lax.ppermute(value, axis, [(i, i ^ flip) for i in range(size)])


def reduced(parts, outer, inner):
    keep_keep, keep_send, send = parts
    got = swap(send, "prow", outer)
    passed = keep_send + got[..., 1, :, :]
    return keep_keep, got[..., 0, :, :], swap(passed, "prow", inner)


def rest_summed(value):
    flip = 4
    while flip < lax.axis_size("prow"):
        got = swap(value, "prow", flip)
        value = value + got
        flip *= 2
    return value


def one_reduced(parts, outer, inner):
    a, b, c = reduced(parts, outer, inner)
    value = a + b + c
    return rest_summed(value)


def two_reduced(even, odd):
    even, odd = reduced(even, 1, 2), reduced(odd, 2, 1)
    value = jnp.stack([a + b + c for a, b, c in (even, odd)])
    return rest_summed(value)


def shared(value):
    return swap(value, "prow", 1), swap(value, "prow", 2)


def body(eigvecs, reflectors, triangles):
    panels, _, width = reflectors.shape
    count = panels // 2
    low, high = bit_of("prow", 0), bit_of("prow", 1)
    scal = jnp.stack([lax.axis_index("prow"), low * 2 + high, high * 2 + low, bit_of("pcol", 1), bit_of("pcol", 0)]).astype(jnp.int32)

    first, turned, early, late = project_first(scal, eigvecs, reflectors, count)
    pairs = pair_products(scal, early, late, width)
    second = project_second(scal, turned, late, width)
    pairs = one_reduced(pairs, 1, 2)
    near0, near1 = shared(pairs)
    diag = swap(pairs, "prow", 3)
    pairs = jnp.concatenate([pairs, near1, near0, diag], 0)
    across = swap(pairs, "pcol", 2)
    quarters = (pairs, across, swap(pairs, "pcol", 1), swap(across, "pcol", 1))
    mine = one_reduced(first, 2, 1)
    near0, near1 = shared(mine)
    folded, joined = fold(scal, quarters, triangles[count:], late)
    blocks = (mine, near0, near1, swap(mine, "prow", 3))
    work, pre = update_middle(scal, blocks, triangles[:count], joined, eigvecs, early)
    mine = two_reduced(*second)
    return update_last(scal, (mine, *shared(mine), swap(mine, "prow", 3)), pre, work, folded)


def solution(mesh):
    in_specs = (P("prow", "pcol"), P(None, "prow", None), P())
    out_specs = P("prow", "pcol")
    return jax.shard_map(body, mesh=mesh, in_specs=in_specs, out_specs=out_specs, check_vma=False)
```
